128 devices in a mesh: gx: 8 (over y, core), gy: 16 (over z, x).
Axes of the slice: x: 4, y: 4, z: 4, core: 2. Of those that a mesh axis runs over, the one named last changes fastest.
Arguments:
- trace_op: bfloat16 [8, 16, 2048, 2048], P('gx', 'gy'), may hold values from -0.125 to 0.125
- src_blocks: bfloat16 [16384, 2048], P(('gx', 'gy')), may hold values from -6 to 6
- src_dest: int32 [16384, 1], P(('gx', 'gy')), may hold values from 0 to 127; in each aligned block of 128 rows (0 to 127, 128 to 255, ...) at most 2 rows name the same one
- src_shot: int32 [16384], P(('gx', 'gy')), may hold values from 0 to 2047
- ret_shot: int32 [128, 128, 4], P(('gx', 'gy')), may hold values from 0 to 2047
- ret_count: int32 [128, 128], P(('gx', 'gy')), may hold values from 0 to 4
Outputs:
- returned: bfloat16 [128, 128, 4, 2048], P(('gx', 'gy'))
The draws below stay inside these ranges and needn't reach their ends.
Inputs may be any that keep to these rules, and one draw needn't show every extreme that they name: `src_dest`: among the rows of one device, no subdomain is named by more than 2 blocks; some subdomain is named by exactly 2.
All inputs are finite; a program needn't handle non-finite values.
Results may differ from the reference program's by a relative error of at most 0.013.
Values may be sent and summed in bfloat16 or wider, within the bound.
A program may use at most 128 MiB of HBM per device.

```python
import math
import jax
import jax.numpy as jnp
import numpy as np
from jax import lax

F = 1024
BLK_DEV = 128
RCAP = 4
SHOTS = 2048
BLOCKS = 16384
SCAP = 2
N_GX = 8
N_GY = 16
DEVICES = 128


def set_ends(drawn, own_key, low, high):
    longest = drawn.shape.index(max(drawn.shape))
    spots = []
    for shift in (0, 1):
        where = [jax.random.randint(jax.random.fold_in(own_key, axis), (), 0, length) for axis, length in enumerate(drawn.shape)]
        where[longest] = (where[longest] + shift) % drawn.shape[longest]
        spots.append(tuple(where))
    return drawn.at[spots[0]].set(low).at[spots[1]].set(high)


def steps_of(key, extent, cuts, smallest, top_value):
    def one(dim, shards_of):
        draws = jax.random.uniform(jax.random.fold_in(jax.random.fold_in(key, 6), dim), (shards_of,), jnp.float32, smallest / len(cuts), top_value / len(cuts))
        return jnp.repeat(jnp.exp(draws), extent[dim] // shards_of).reshape((-1,) + (1,) * (len(extent) - dim - 1))

    loudness = one(*cuts[0])
    for cut in cuts[1:]:
        loudness = loudness * one(*cut)
    return loudness


def routed_block(key, own, number, rows, number_of, top, reach, lean):
    ranking = jax.random.permutation(key, number_of)
    heavy_load, usual = shares(number_of, rows * top, reach, lean, True), shares(number_of, rows * top, reach, lean, False)
    places = jnp.arange(number_of)

    def named(lengths, turn):
        used = int((lengths > 0).sum())
        fixed = max(1, used // 4)
        passed = fixed + (places - fixed + turn * (used - fixed)) % max(1, number_of - fixed)
        return jnp.zeros((number_of,), jnp.int32).at[ranking[jnp.where(places < fixed, places, passed)]].set(jnp.asarray(lengths, jnp.int32))

    lengths = jnp.where(number % 4 == 0, named(heavy_load, number // 4), named(usual, number - number // 4 - 1))
    mixed = jax.random.permutation(jax.random.fold_in(own, 3), number_of)
    donor, sink = mixed[0:number_of // 2 * 2:2], mixed[1:number_of // 2 * 2:2]
    margin = jnp.minimum(lengths[donor] - 1, reach - lengths[sink]) // 2
    margin = jnp.where((donor == ranking[0]) | (sink == ranking[0]) | (lengths[sink] == 0), 0, jnp.maximum(margin, 0))
    passed = jax.random.randint(jax.random.fold_in(own, 4), (number_of // 2,), 0, 1 << 20) % (margin + 1)
    lengths = lengths.at[donor].add(-passed).at[sink].add(passed)
    items = jnp.searchsorted(jnp.cumsum(lengths), jnp.arange(rows * top), side="right").astype(jnp.int32)
    grid = items.reshape(top, rows).T
    grid = grid[jax.random.permutation(jax.random.fold_in(own, 1), rows)]
    turn = jax.random.randint(jax.random.fold_in(own, 2), (rows, 1), 0, top)
    return jnp.take_along_axis(grid, (jnp.arange(top)[None, :] + turn) % top, axis=1)


def shares(number_of, total, bound, skew, full):
    weights = [(1 << 20) // math.isqrt(grade ** skew) + 1 for grade in range(1, number_of + 1)]
    largest = bound if full else min(bound, max(-(-total // number_of), total * weights[0] // sum(weights)))
    least = 1 if total - largest >= number_of - 1 else 0
    given, spare = [largest] + [least] * (number_of - 1), total - largest - least * (number_of - 1)
    while spare > 0:
        movable = [i for i in range(1, number_of) if given[i] < largest] or [i for i in range(1, number_of) if given[i] < bound]
        pool, left = sum([weights[i] for i in movable]), spare
        for i in movable:
            more = min(bound - given[i], max(1, left * weights[i] // pool), spare)
            given[i] = given[i] + more
            spare = spare - more
    return np.array(given)


def centred(own_key, extent, scale, most, split=(), kind=jnp.bfloat16):
    loudness = steps_of(own_key, extent, split, -0.22, 0.18) if split else 1.0
    drawn = jax.random.normal(own_key, extent, jnp.float32) * scale * loudness
    return jnp.minimum(jnp.maximum(drawn, -most), most).astype(kind)


def setup_inputs(seed: int = 0) -> dict:
    key_list = jax.random.split(jax.random.key(seed), 7)
    trace_op = centred(key_list[0], (N_GX, N_GY, 2 * F, 2 * F), (2 * F) ** -0.5, 0.125, ((0, 8), (1, 16)))
    src_blocks = centred(key_list[1], (BLOCKS, 2 * F), 1.0, 6.0, ((0, 128),))
    src_dest_keys = jax.random.split(jax.random.fold_in(key_list[2], 1), BLOCKS // BLK_DEV)
    src_dest_turns = jax.random.permutation(jax.random.fold_in(key_list[2], 3), BLOCKS // BLK_DEV)
    src_dest = jax.vmap(lambda own, number: routed_block(jax.random.fold_in(key_list[2], 2), own, number, BLK_DEV, DEVICES, 1, SCAP, 2))(src_dest_keys, src_dest_turns).reshape((BLOCKS, 1))
    src_shot = set_ends(jax.random.randint(key_list[3], (BLOCKS,), 0, SHOTS), jax.random.fold_in(key_list[3], 1), 0, SHOTS - 1).astype(jnp.int32)
    ret_shot = set_ends(jax.random.randint(key_list[4], (DEVICES, DEVICES, RCAP), 0, SHOTS), jax.random.fold_in(key_list[4], 1), 0, SHOTS - 1).astype(jnp.int32)
    ret_count = set_ends(jax.random.randint(key_list[5], (DEVICES, DEVICES), 0, RCAP + 1), jax.random.fold_in(key_list[5], 1), 0, RCAP).astype(jnp.int32)
    return dict(trace_op=trace_op, src_blocks=src_blocks, src_dest=src_dest, src_shot=src_shot, ret_shot=ret_shot, ret_count=ret_count)


def reference(trace_op, src_blocks, src_dest, src_shot, ret_shot, ret_count):
    flat = (src_dest[:, 0] * SHOTS + src_shot).astype(jnp.int32)
    source = jax.ops.segment_sum(src_blocks.astype(jnp.float32), flat, num_segments=DEVICES * SHOTS)
    source = source.reshape(N_GX, N_GY, SHOTS, 2 * F)

    def column(left_faces, inputs):
        operators, sources = inputs

        def cell(lower, items):
            operator, term, left = items
            total = jnp.dot(left, operator[:F], preferred_element_type=jnp.float32)
            total = total + jnp.dot(lower, operator[F:], preferred_element_type=jnp.float32)
            result = (total + term).astype(jnp.bfloat16)
            return result[:, F:], result

        start = jnp.zeros((SHOTS, F), jnp.bfloat16)
        _, outputs = lax.scan(cell, start, (operators, sources, left_faces))
        return outputs[:, :, :F], outputs

    begin = jnp.zeros((N_GY, SHOTS, F), jnp.bfloat16)
    _, traces = lax.scan(column, begin, (trace_op, source))
    traces = traces.reshape(DEVICES, SHOTS, 2 * F)
    owners = jnp.arange(DEVICES, dtype=jnp.int32)[:, None, None]
    picked = traces[owners, ret_shot]
    live = jnp.arange(RCAP, dtype=jnp.int32)[None, None, :] < ret_count[:, :, None]
    picked = jnp.where(live[..., None], picked, jnp.zeros_like(picked))
    return jnp.transpose(picked, (1, 0, 2, 3))
```

```python
import functools

import jax
import jax.numpy as jnp
from jax import lax
from jax.experimental import pallas as pl
from jax.experimental.pallas import tpu as pltpu
from jax.sharding import PartitionSpec as P

MESH = pl.DeviceIdType.MESH
CHUNK = 32
RCAP = 4


def sweep(cols, rows, w_hbm, blocks, shots, want, out, w, xbuf, traces, wsem, send_r, recv_r, send_u, recv_u):
    i = lax.axis_index("gx")
    j = lax.axis_index("gy")
    total, width = traces.shape
    face = width // 2
    slots = blocks.shape[0]
    chunks = total // CHUNK
    load = pltpu.make_async_copy(w_hbm, w.at[pl.ds(0, width)], wsem)
    load.start()
    w[pl.ds(width, slots)] = blocks[...]

    @pl.when(i == 0)
    def _():
        xbuf[:, :face] = jnp.zeros((total, face), jnp.bfloat16)

    @pl.when(j == 0)
    def _():
        xbuf[:, face:] = jnp.zeros((total, face), jnp.bfloat16)

    load.wait()

    def right(k):
        at = pl.ds(pl.multiple_of(k * CHUNK, CHUNK), CHUNK)
        return pltpu.make_async_remote_copy(
            src_ref=traces.at[at, pl.ds(0, face)],
            dst_ref=xbuf.at[at, pl.ds(0, face)],
            send_sem=send_r.at[k],
            recv_sem=recv_r.at[k],
            device_id={"gx": lax.rem(i + 1, cols)},
            device_id_type=MESH,
        )

    def upper(k):
        at = pl.ds(pl.multiple_of(k * CHUNK, CHUNK), CHUNK)
        return pltpu.make_async_remote_copy(
            src_ref=traces.at[at, pl.ds(face, face)],
            dst_ref=xbuf.at[at, pl.ds(face, face)],
            send_sem=send_u.at[k],
            recv_sem=recv_u.at[k],
            device_id={"gy": lax.rem(j + 1, rows)},
            device_id_type=MESH,
        )

    def step(k, _):
        at = pl.ds(pl.multiple_of(k * CHUNK, CHUNK), CHUNK)
        number = lax.broadcasted_iota(jnp.int32, (CHUNK, slots), 0) + k * CHUNK
        pick = jnp.where(number == shots[...], 1.0, 0.0).astype(jnp.bfloat16)

        @pl.when(i > 0)
        def _():
            right(k).wait_recv()

        @pl.when(j > 0)
        def _():
            upper(k).wait_recv()

        x = jnp.concatenate([xbuf[at, :], pick], axis=1)
        traces[at, face:] = jnp.dot(x, w[:, face:], preferred_element_type=jnp.float32).astype(jnp.bfloat16)

        @pl.when(j < rows - 1)
        def _():
            upper(k).start()

        traces[at, :face] = jnp.dot(x, w[:, :face], preferred_element_type=jnp.float32).astype(jnp.bfloat16)

        @pl.when(i < cols - 1)
        def _():
            right(k).start()

        return 0

    lax.fori_loop(0, chunks, step, 0)
    number = lax.broadcasted_iota(jnp.int32, (128, total), 1)
    for part in range(want.shape[0] // 128):
        rows_at = pl.ds(part * 128, 128)
        pick = jnp.where(number == want[rows_at, :], 1.0, 0.0).astype(jnp.bfloat16)
        for piece in range(4):
            c = pl.ds(piece * (width // 4), width // 4)
            out[rows_at, c] = jnp.dot(pick, traces[:, c], preferred_element_type=jnp.float32).astype(jnp.bfloat16)

    def drain(k, _):
        @pl.when(j < rows - 1)
        def _():
            upper(k).wait_send()

        @pl.when(i < cols - 1)
        def _():
            right(k).wait_send()

        return 0

    lax.fori_loop(0, chunks, drain, 0)


def body(trace_op, src_blocks, src_dest, src_shot, ret_shot, ret_count):
    cols = lax.axis_size("gx")
    rows = lax.axis_size("gy")
    ndev = cols * rows
    blk, width = src_blocks.shape
    shots = 2048
    scap = max(2, 2 * blk // ndev)
    dest = src_dest[:, 0]
    hits = (dest[:, None] == jnp.arange(ndev, dtype=jnp.int32)[None, :]).astype(jnp.int32)
    ranks = jnp.sum((jnp.cumsum(hits, axis=0) - 1) * hits, axis=1)
    target = dest * scap + ranks
    place = jnp.arange(ndev * scap, dtype=jnp.int32)[:, None] == target[None, :]
    packed = jnp.dot(
        place.astype(jnp.bfloat16), src_blocks, preferred_element_type=jnp.float32
    ).astype(jnp.bfloat16)
    slot_shots = jnp.max(jnp.where(place, src_shot[None, :], -1), axis=1)
    recv_blocks = lax.all_to_all(
        packed.reshape(ndev, scap, width), ("gx", "gy"), split_axis=0, concat_axis=0, tiled=True
    ).reshape(ndev * scap, width)
    recv_shots = lax.all_to_all(
        slot_shots.reshape(ndev, scap), ("gx", "gy"), split_axis=0, concat_axis=0, tiled=True
    ).reshape(1, ndev * scap)
    live = jnp.arange(RCAP, dtype=jnp.int32)[None, :] < ret_count.reshape(ndev, 1)
    want = jnp.where(live, ret_shot.reshape(ndev, RCAP), -1).reshape(ndev * RCAP, 1)
    vmem = pl.BlockSpec(memory_space=pltpu.VMEM)
    chunks = shots // CHUNK
    chosen = pl.pallas_call(
        functools.partial(sweep, cols, rows),
        out_shape=jax.ShapeDtypeStruct((ndev * RCAP, width), jnp.bfloat16),
        in_specs=[pl.BlockSpec(memory_space=pl.ANY), vmem, vmem, vmem],
        out_specs=vmem,
        scratch_shapes=[
            pltpu.VMEM((width + ndev * scap, width), jnp.bfloat16),
            pltpu.VMEM((shots, width), jnp.bfloat16),
            pltpu.VMEM((shots, width), jnp.bfloat16),
            pltpu.SemaphoreType.DMA,
            pltpu.SemaphoreType.DMA((chunks,)),
            pltpu.SemaphoreType.DMA((chunks,)),
            pltpu.SemaphoreType.DMA((chunks,)),
            pltpu.SemaphoreType.DMA((chunks,)),
        ],
        compiler_params=pltpu.CompilerParams(has_side_effects=True, vmem_limit_bytes=60 * 1024 * 1024),
    )(trace_op.reshape(width, width), recv_blocks, recv_shots, want)
    arrived = lax.all_to_all(
        chosen.reshape(ndev, RCAP, width), ("gx", "gy"), split_axis=0, concat_axis=0, tiled=True
    )
    return arrived.reshape(1, ndev, RCAP, width)


def solution(mesh):
    in_specs = (
        P("gx", "gy", None, None),
        P(("gx", "gy"), None),
        P(("gx", "gy"), None),
        P(("gx", "gy")),
        P(("gx", "gy"), None, None),
        P(("gx", "gy"), None),
    )
    out_specs = P(("gx", "gy"), None, None, None)
    return jax.shard_map(body, mesh=mesh, in_specs=in_specs, out_specs=out_specs, check_vma=False)
```

```python
import functools

import jax
import jax.numpy as jnp
from jax import lax
from jax.experimental import pallas as pl
from jax.experimental.pallas import tpu as pltpu
from jax.sharding import PartitionSpec as P

MESH = pl.DeviceIdType.MESH
CHUNK = 32
RCAP = 4
LANES = 128


def mega(cols, rows, w_hbm, src, dest_c, dest_r, shot_r, want, out,
         w, xbuf, traces, sbuf, rbuf, gbuf, shots, wsem, ssem, rsem, lsem, gsem, osem, psem,
         send_r, recv_r, send_u, recv_u):
    i = lax.axis_index("gx")
    j = lax.axis_index("gy")
    ndev = cols * rows
    me = i * rows + j
    total, width = traces.shape
    face = width // 2
    scap = sbuf.shape[1]
    slots = ndev * scap
    blk = src.shape[0]
    chunks = total // CHUNK
    load = pltpu.make_async_copy(w_hbm, w.at[pl.ds(0, width)], wsem)
    load.start()

    same = dest_c[...] == dest_r[...]
    earlier = lax.broadcasted_iota(jnp.int32, (blk, blk), 0) < lax.broadcasted_iota(jnp.int32, (blk, blk), 1)
    rank = jnp.sum(jnp.where(same & earlier, 1, 0), axis=0, keepdims=True)
    target = dest_r[...] * scap + rank
    place = lax.broadcasted_iota(jnp.int32, (slots, blk), 0) == target
    tag = jnp.sum(jnp.where(place, shot_r[...] + 1, 0), axis=1, keepdims=True)
    lane = lax.broadcasted_iota(jnp.int32, (slots, LANES), 1)
    extra = jnp.where(lane == 0, lax.shift_right_logical(tag, 6), jnp.where(lane == 1, tag & 63, 0))
    place = jnp.where(place, 1.0, 0.0).astype(jnp.bfloat16)
    for c in range(0, width, 512):
        part = jnp.dot(place, src[:, c:c + 512], preferred_element_type=jnp.float32).astype(jnp.bfloat16)
        sbuf[:, :, c:c + 512] = part.reshape(ndev, scap, 512)
    sbuf[:, :, width:] = extra.astype(jnp.float32).astype(jnp.bfloat16).reshape(ndev, scap, LANES)

    def block(a, b):
        return pltpu.make_async_remote_copy(
            src_ref=sbuf.at[a * rows + b], dst_ref=rbuf.at[me], send_sem=ssem, recv_sem=rsem,
            device_id=(a, b), device_id_type=MESH,
        )

    def post(t, _):
        a = lax.rem(t + i, cols)
        b = t // cols - a

        @pl.when((b >= 0) & (b < rows) & ((a != i) | (b != j)))
        def _():
            block(a, b).start()

        return 0

    lax.fori_loop(0, (cols + rows - 1) * cols, post, 0)
    own = pltpu.make_async_copy(sbuf.at[me], rbuf.at[me], lsem)
    own.start()

    @pl.when(i == 0)
    def _():
        xbuf[:, :face] = jnp.zeros((total, face), jnp.bfloat16)

    @pl.when(j == 0)
    def _():
        xbuf[:, face:] = jnp.zeros((total, face), jnp.bfloat16)

    own.wait()
    pltpu.make_async_copy(rbuf.at[pl.ds(0, ndev - 1)], rbuf.at[pl.ds(0, ndev - 1)], rsem).wait()
    for c in range(0, width, 512):
        w[width:, c:c + 512] = rbuf[:, :, c:c + 512].reshape(slots, 512)
    code = rbuf[:, :, width:].reshape(slots, LANES).astype(jnp.float32)
    code = jnp.transpose(code)
    shots[...] = (code[0:1, :] * 64.0 + code[1:2, :] - 1.0).astype(jnp.int32)
    load.wait()

    def right(k):
        at = pl.ds(pl.multiple_of(k * CHUNK, CHUNK), CHUNK)
        return pltpu.make_async_remote_copy(
            src_ref=traces.at[at, pl.ds(0, face)],
            dst_ref=xbuf.at[at, pl.ds(0, face)],
            send_sem=send_r.at[k],
            recv_sem=recv_r.at[k],
            device_id=(lax.rem(i + 1, cols), j),
            device_id_type=MESH,
        )

    def upper(k):
        at = pl.ds(pl.multiple_of(k * CHUNK, CHUNK), CHUNK)
        return pltpu.make_async_remote_copy(
            src_ref=traces.at[at, pl.ds(face, face)],
            dst_ref=xbuf.at[at, pl.ds(face, face)],
            send_sem=send_u.at[k],
            recv_sem=recv_u.at[k],
            device_id=(i, lax.rem(j + 1, rows)),
            device_id_type=MESH,
        )

    def step(k, _):
        at = pl.ds(pl.multiple_of(k * CHUNK, CHUNK), CHUNK)
        number = lax.broadcasted_iota(jnp.int32, (CHUNK, slots), 0) + k * CHUNK
        pick = jnp.where(number == shots[...], 1.0, 0.0).astype(jnp.bfloat16)

        @pl.when(i > 0)
        def _():
            right(k).wait_recv()

        @pl.when(j > 0)
        def _():
            upper(k).wait_recv()

        x = jnp.concatenate([xbuf[at, :], pick], axis=1)
        traces[at, face:] = jnp.dot(x, w[:, face:], preferred_element_type=jnp.float32).astype(jnp.bfloat16)

        @pl.when(j < rows - 1)
        def _():
            upper(k).start()

        traces[at, :face] = jnp.dot(x, w[:, :face], preferred_element_type=jnp.float32).astype(jnp.bfloat16)

        @pl.when(i < cols - 1)
        def _():
            right(k).start()

        return 0

    lax.fori_loop(0, chunks, step, 0)

    def answer(o):
        return pltpu.make_async_remote_copy(
            src_ref=gbuf.at[o], dst_ref=out.at[me], send_sem=gsem, recv_sem=osem,
            device_id=(o // rows, lax.rem(o, rows)), device_id_type=MESH,
        )

    owners = 32
    parts = ndev // owners
    number = lax.broadcasted_iota(jnp.int32, (owners * RCAP, total), 1)

    def gather(t, _):
        part = lax.rem(t + me // owners, parts)
        rows_at = pl.ds(pl.multiple_of(part * owners * RCAP, owners * RCAP), owners * RCAP)
        base = pl.multiple_of(part * owners, owners)
        pick = jnp.where(number == want[rows_at, :], 1.0, 0.0).astype(jnp.bfloat16)
        for c in range(0, width, 512):
            got = jnp.dot(pick, traces[:, c:c + 512], preferred_element_type=jnp.float32).astype(jnp.bfloat16)
            gbuf[pl.ds(base, owners), :, c:c + 512] = got.reshape(owners, RCAP, 512)

        def reply(q, _):
            o = base + lax.rem(q + me, owners)

            @pl.when(o != me)
            def _():
                answer(o).start()

            return 0

        lax.fori_loop(0, owners, reply, 0)
        return 0

    lax.fori_loop(0, parts, gather, 0)
    mine = pltpu.make_async_copy(gbuf.at[me], out.at[me], psem)
    mine.start()

    def drain(k, _):
        @pl.when(j < rows - 1)
        def _():
            upper(k).wait_send()

        @pl.when(i < cols - 1)
        def _():
            right(k).wait_send()

        return 0

    lax.fori_loop(0, chunks, drain, 0)
    most = pl.ds(0, ndev - 1)
    pltpu.make_async_copy(sbuf.at[most], sbuf.at[most], ssem).wait()
    pltpu.make_async_copy(gbuf.at[most], gbuf.at[most], gsem).wait()
    mine.wait()
    pltpu.make_async_copy(out.at[most], out.at[most], osem).wait()


def body(trace_op, src_blocks, src_dest, src_shot, ret_shot, ret_count):
    cols = lax.axis_size("gx")
    rows = lax.axis_size("gy")
    ndev = cols * rows
    blk, width = src_blocks.shape
    total = 2048
    scap = 2
    live = jnp.arange(RCAP, dtype=jnp.int32)[None, :] < ret_count.reshape(ndev, 1)
    want = jnp.where(live, ret_shot.reshape(ndev, RCAP), -1).reshape(ndev * RCAP, 1)
    vmem = pl.BlockSpec(memory_space=pltpu.VMEM)
    hbm = pl.BlockSpec(memory_space=pl.ANY)
    chunks = total // CHUNK
    dma = pltpu.SemaphoreType.DMA
    arrived = pl.pallas_call(
        functools.partial(mega, cols, rows),
        out_shape=jax.ShapeDtypeStruct((ndev, RCAP, width), jnp.bfloat16),
        in_specs=[hbm, vmem, vmem, vmem, vmem, vmem],
        out_specs=hbm,
        scratch_shapes=[
            pltpu.VMEM((width + ndev * scap, width), jnp.bfloat16),
            pltpu.VMEM((total, width), jnp.bfloat16),
            pltpu.VMEM((total, width), jnp.bfloat16),
            pltpu.VMEM((ndev, scap, width + LANES), jnp.bfloat16),
            pltpu.VMEM((ndev, scap, width + LANES), jnp.bfloat16),
            pltpu.VMEM((ndev, RCAP, width), jnp.bfloat16),
            pltpu.VMEM((1, ndev * scap), jnp.int32),
            dma, dma, dma, dma, dma, dma, dma,
            dma((chunks,)), dma((chunks,)), dma((chunks,)), dma((chunks,)),
        ],
        compiler_params=pltpu.CompilerParams(has_side_effects=True, vmem_limit_bytes=60 * 1024 * 1024),
    )(
        trace_op.reshape(width, width),
        src_blocks,
        src_dest,
        src_dest.reshape(1, blk),
        src_shot.reshape(1, blk),
        want,
    )
    return arrived.reshape(1, ndev, RCAP, width)


def solution(mesh):
    in_specs = (
        P("gx", "gy", None, None),
        P(("gx", "gy"), None),
        P(("gx", "gy"), None),
        P(("gx", "gy")),
        P(("gx", "gy"), None, None),
        P(("gx", "gy"), None),
    )
    out_specs = P(("gx", "gy"), None, None, None)
    return jax.shard_map(body, mesh=mesh, in_specs=in_specs, out_specs=out_specs, check_vma=False)
```

```python
import functools

import jax
import jax.numpy as jnp
from jax import lax
from jax.experimental import pallas as pl
from jax.experimental.pallas import tpu as pltpu
from jax.sharding import PartitionSpec as P

MESH = pl.DeviceIdType.MESH
CHUNK = 48
SPAN = 384
MARK = 3
BAND = 4
RCAP = 4
LANES = 128


def mega(cols, rows, total, w_hbm, src, dest_r, shot_r, ret, count, out,
         w, xbuf, traces, sbuf, rbuf, gbuf, acc, want, shots, gate, wsem, ssem, rsem, lsem, gsem, osem, psem,
         send_r, recv_r, send_u, recv_u):
    i = lax.axis_index("gx")
    j = lax.axis_index("gy")
    ndev = cols * rows
    me = i * rows + j
    padded, width = traces.shape
    face = width // 2
    scap = sbuf.shape[1]
    slots = ndev * scap
    blk = src.shape[0]
    chunks = padded // CHUNK
    load = pltpu.make_async_copy(w_hbm, w.at[pl.ds(0, width)], wsem)
    load.start()

    dest_c = jnp.transpose(jnp.broadcast_to(dest_r[...].astype(jnp.float32), (blk, blk)))
    same = dest_c == dest_r[...].astype(jnp.float32)
    earlier = lax.broadcasted_iota(jnp.int32, (blk, blk), 0) < lax.broadcasted_iota(jnp.int32, (blk, blk), 1)
    rank = jnp.sum(jnp.where(same & earlier, 1, 0), axis=0, keepdims=True)
    target = dest_r[...] * scap + rank
    place = lax.broadcasted_iota(jnp.int32, (slots, blk), 0) == target
    tag = jnp.sum(jnp.where(place, shot_r[...] + 1, 0), axis=1, keepdims=True)
    lane = lax.broadcasted_iota(jnp.int32, (slots, LANES), 1)
    extra = jnp.where(lane == 0, lax.shift_right_logical(tag, 6), jnp.where(lane == 1, tag & 63, 0))
    place = jnp.where(place, 1.0, 0.0).astype(jnp.bfloat16)
    for c in range(0, width, 512):
        part = jnp.dot(place, src[:, c:c + 512], preferred_element_type=jnp.float32).astype(jnp.bfloat16)
        sbuf[:, :, c:c + 512] = part.reshape(ndev, scap, 512)
    sbuf[:, :, width:] = extra.astype(jnp.float32).astype(jnp.bfloat16).reshape(ndev, scap, LANES)

    def block(a, b):
        return pltpu.make_async_remote_copy(
            src_ref=sbuf.at[a * rows + b], dst_ref=rbuf.at[me], send_sem=ssem, recv_sem=rsem,
            device_id=(a, b), device_id_type=MESH,
        )

    def post(t, _):
        a = lax.rem(t + i, cols)
        b = t // cols - a

        @pl.when((b >= 0) & (b < rows) & ((a != i) | (b != j)))
        def _():
            block(a, b).start()

        return 0

    lax.fori_loop(0, (cols + rows - 1) * cols, post, 0)
    own = pltpu.make_async_copy(sbuf.at[me], rbuf.at[me], lsem)
    own.start()

    slot = lax.broadcasted_iota(jnp.int32, (RCAP, ndev), 0)
    asked = jnp.where(slot < count[...], ret[...] + 1, 0)
    split = jnp.concatenate(
        [lax.shift_right_logical(asked, 6), asked & 63, jnp.zeros((ndev - 2 * RCAP, ndev), jnp.int32)], axis=0
    ).astype(jnp.float32)
    split = jnp.transpose(split).astype(jnp.bfloat16)
    asks = ndev * RCAP
    row = lax.broadcasted_iota(jnp.int32, (asks, ndev), 0)
    lane = lax.broadcasted_iota(jnp.int32, (asks, ndev), 1)
    place = row // RCAP
    owner = (place // BAND % cols) * rows + place // (BAND * cols) * BAND + place % BAND
    spread = jnp.where(lane == owner, 1.0, 0.0).astype(jnp.bfloat16)
    spread = jnp.dot(spread, split, preferred_element_type=jnp.float32)
    spread = jnp.where(lane == row % RCAP, spread * 64.0, jnp.where(lane == row % RCAP + RCAP, spread, 0.0))
    want[...] = jnp.sum(spread, axis=1, keepdims=True).astype(jnp.int32) - 1
    acc[...] = jnp.zeros_like(acc)

    @pl.when(i == 0)
    def _():
        xbuf[:, :face] = jnp.zeros((padded, face), jnp.bfloat16)

    @pl.when(j == 0)
    def _():
        xbuf[:, face:] = jnp.zeros((padded, face), jnp.bfloat16)

    own.wait()
    pltpu.make_async_copy(rbuf.at[pl.ds(0, ndev - 1)], rbuf.at[pl.ds(0, ndev - 1)], rsem).wait()
    for c in range(0, width, 512):
        w[width:, c:c + 512] = rbuf[:, :, c:c + 512].reshape(slots, 512)
    code = rbuf[:, :, width:].reshape(slots, LANES).astype(jnp.float32)
    code = jnp.transpose(code)
    shots[...] = (code[0:1, :] * 64.0 + code[1:2, :] - 1.0).astype(jnp.int32)
    load.wait()

    def right(k):
        at = pl.ds(pl.multiple_of(k * CHUNK, CHUNK), CHUNK)
        return pltpu.make_async_remote_copy(
            src_ref=traces.at[at, pl.ds(0, face)],
            dst_ref=xbuf.at[at, pl.ds(0, face)],
            send_sem=send_r.at[k],
            recv_sem=recv_r.at[k],
            device_id=(lax.rem(i + 1, cols), j),
            device_id_type=MESH,
        )

    def upper(k):
        at = pl.ds(pl.multiple_of(k * CHUNK, CHUNK), CHUNK)
        return pltpu.make_async_remote_copy(
            src_ref=traces.at[at, pl.ds(face, face)],
            dst_ref=xbuf.at[at, pl.ds(face, face)],
            send_sem=send_u.at[k],
            recv_sem=recv_u.at[k],
            device_id=(i, lax.rem(j + 1, rows)),
            device_id_type=MESH,
        )

    def step(k, _):
        at = pl.ds(pl.multiple_of(k * CHUNK, CHUNK), CHUNK)
        number = lax.broadcasted_iota(jnp.int32, (CHUNK, slots), 0) + k * CHUNK
        pick = jnp.where(number == shots[...], 1.0, 0.0).astype(jnp.bfloat16)

        @pl.when(i > 0)
        def _():
            right(k).wait_recv()

        @pl.when(j > 0)
        def _():
            upper(k).wait_recv()

        x = jnp.concatenate([xbuf[at, :], pick], axis=1)
        traces[at, face:] = jnp.dot(x, w[:, face:], preferred_element_type=jnp.float32).astype(jnp.bfloat16)

        @pl.when(j < rows - 1)
        def _():
            upper(k).start()

        traces[at, :face] = jnp.dot(x, w[:, :face], preferred_element_type=jnp.float32).astype(jnp.bfloat16)

        @pl.when(i < cols - 1)
        def _():
            right(k).start()

        @pl.when(lax.rem(k, SPAN // CHUNK) == SPAN // CHUNK - 1)
        def _():
            first = pl.multiple_of((k // (SPAN // CHUNK)) * SPAN, SPAN)
            number = lax.broadcasted_iota(jnp.int32, (asks, SPAN), 1) + first
            pick = jnp.where(number == want[...], 1.0, 0.0).astype(jnp.bfloat16)
            for c in range(0, width, 256):
                got = jnp.dot(pick, traces[pl.ds(first, SPAN), c:c + 256], preferred_element_type=jnp.float32)
                acc[:, c:c + 256] += got.astype(jnp.bfloat16)

        return 0

    lax.fori_loop(0, chunks, step, 0)

    def answer(q, a, b):
        return pltpu.make_async_remote_copy(
            src_ref=gbuf.at[q], dst_ref=out.at[me], send_sem=gsem, recv_sem=osem,
            device_id=(a, b), device_id_type=MESH,
        )

    @pl.when((i == MARK) & (lax.rem(j, BAND) == BAND - 1))
    def _():
        def tell(p, _):
            @pl.when(p != me)
            def _():
                pl.semaphore_signal(
                    gate.at[j // BAND], inc=1, device_id=(p // rows, lax.rem(p, rows)), device_id_type=MESH
                )

            return 0

        lax.fori_loop(0, ndev, tell, 0)
        pl.semaphore_signal(gate.at[j // BAND], inc=1)

    last = total // SPAN * SPAN
    owners = BAND * cols
    number = lax.broadcasted_iota(jnp.int32, (owners * RCAP, total - last), 1) + last

    def finish(g, _):
        rows_at = pl.ds(pl.multiple_of(g * owners * RCAP, owners * RCAP), owners * RCAP)
        pick = jnp.where(number == want[rows_at, :], 1.0, 0.0).astype(jnp.bfloat16)
        for c in range(0, width, 512):
            got = jnp.dot(pick, traces[last:total, c:c + 512], preferred_element_type=jnp.float32).astype(jnp.bfloat16)
            got = got + acc[rows_at, c:c + 512]
            gbuf[pl.ds(pl.multiple_of(g * owners, owners), owners), :, c:c + 512] = got.reshape(owners, RCAP, 512)
        pl.semaphore_wait(gate.at[g], 1)

        def reply(q, _):
            t = lax.rem(q + me, owners)
            a = t // BAND
            b = g * BAND + lax.rem(t, BAND)

            @pl.when((a != i) | (b != j))
            def _():
                answer(g * owners + t, a, b).start()

            return 0

        lax.fori_loop(0, owners, reply, 0)
        return 0

    lax.fori_loop(0, rows // BAND, finish, 0)
    home = (j // BAND) * owners + i * BAND + lax.rem(j, BAND)
    mine = pltpu.make_async_copy(gbuf.at[home], out.at[me], psem)
    mine.start()

    def drain(k, _):
        @pl.when(j < rows - 1)
        def _():
            upper(k).wait_send()

        @pl.when(i < cols - 1)
        def _():
            right(k).wait_send()

        return 0

    lax.fori_loop(0, chunks, drain, 0)
    most = pl.ds(0, ndev - 1)
    pltpu.make_async_copy(sbuf.at[most], sbuf.at[most], ssem).wait()
    pltpu.make_async_copy(gbuf.at[most], gbuf.at[most], gsem).wait()
    mine.wait()
    pltpu.make_async_copy(out.at[most], out.at[most], osem).wait()


def body(trace_op, src_blocks, src_dest, src_shot, ret_shot, ret_count):
    cols = lax.axis_size("gx")
    rows = lax.axis_size("gy")
    ndev = cols * rows
    blk, width = src_blocks.shape
    total = 2048
    scap = 2
    vmem = pl.BlockSpec(memory_space=pltpu.VMEM)
    hbm = pl.BlockSpec(memory_space=pl.ANY)
    chunks = pl.cdiv(total, CHUNK)
    padded = chunks * CHUNK
    dma = pltpu.SemaphoreType.DMA
    arrived = pl.pallas_call(
        functools.partial(mega, cols, rows, total),
        out_shape=jax.ShapeDtypeStruct((ndev, RCAP, width), jnp.bfloat16),
        in_specs=[hbm, vmem, vmem, vmem, vmem, vmem],
        out_specs=hbm,
        scratch_shapes=[
            pltpu.VMEM((width + ndev * scap, width), jnp.bfloat16),
            pltpu.VMEM((padded, width), jnp.bfloat16),
            pltpu.VMEM((padded, width), jnp.bfloat16),
            pltpu.VMEM((ndev, scap, width + LANES), jnp.bfloat16),
            pltpu.VMEM((ndev, scap, width + LANES), jnp.bfloat16),
            pltpu.VMEM((ndev, RCAP, width), jnp.bfloat16),
            pltpu.VMEM((ndev * RCAP, width), jnp.bfloat16),
            pltpu.VMEM((ndev * RCAP, 1), jnp.int32),
            pltpu.VMEM((1, ndev * scap), jnp.int32),
            pltpu.SemaphoreType.REGULAR((rows // BAND,)),
            dma, dma, dma, dma, dma, dma, dma,
            dma((chunks,)), dma((chunks,)), dma((chunks,)), dma((chunks,)),
        ],
        compiler_params=pltpu.CompilerParams(has_side_effects=True, vmem_limit_bytes=60 * 1024 * 1024),
    )(
        trace_op.reshape(width, width),
        src_blocks,
        src_dest.reshape(1, blk),
        src_shot.reshape(1, blk),
        ret_shot.reshape(ndev, RCAP).T,
        ret_count.reshape(1, ndev),
    )
    return arrived.reshape(1, ndev, RCAP, width)


def solution(mesh):
    in_specs = (
        P("gx", "gy", None, None),
        P(("gx", "gy"), None),
        P(("gx", "gy"), None),
        P(("gx", "gy")),
        P(("gx", "gy"), None, None),
        P(("gx", "gy"), None),
    )
    out_specs = P(("gx", "gy"), None, None, None)
    return jax.shard_map(body, mesh=mesh, in_specs=in_specs, out_specs=out_specs, check_vma=False)
```

```python
import functools

import jax
import jax.numpy as jnp
from jax import lax
from jax.experimental import pallas as pl
from jax.experimental.pallas import tpu as pltpu
from jax.sharding import PartitionSpec as P

MESH = pl.DeviceIdType.MESH
CHUNK = 48
SPAN = 384
MARK = 5
BAND = 4
RCAP = 4
LANES = 128


def mega(cols, rows, total, w_hbm, src, dest_r, shot_r, ret, count, out,
         w, xbuf, traces, sbuf, rbuf, gbuf, acc, want, shots, held, gate, wsem, ssem, rsem, lsem, gsem, osem, psem,
         send_r, recv_r, send_u, recv_u):
    i = lax.axis_index("gx")
    j = lax.axis_index("gy")
    ndev = cols * rows
    me = i * rows + j
    padded, width = traces.shape
    face = width // 2
    scap = sbuf.shape[1]
    slots = ndev * scap
    blk = src.shape[0]
    chunks = padded // CHUNK
    load = pltpu.make_async_copy(w_hbm, w.at[pl.ds(0, width)], wsem)
    load.start()
    barrier = pltpu.get_barrier_semaphore()

    def greet(p, _):
        @pl.when(p != me)
        def _():
            pl.semaphore_signal(barrier, inc=1, device_id=(p // rows, lax.rem(p, rows)), device_id_type=MESH)

        return 0

    lax.fori_loop(0, ndev, greet, 0)

    dest_c = jnp.transpose(jnp.broadcast_to(dest_r[...].astype(jnp.float32), (blk, blk)))
    same = dest_c == dest_r[...].astype(jnp.float32)
    earlier = lax.broadcasted_iota(jnp.int32, (blk, blk), 0) < lax.broadcasted_iota(jnp.int32, (blk, blk), 1)
    rank = jnp.sum(jnp.where(same & earlier, 1, 0), axis=0, keepdims=True)
    target = dest_r[...] * scap + rank
    place = lax.broadcasted_iota(jnp.int32, (slots, blk), 0) == target
    tag = jnp.sum(jnp.where(place, shot_r[...] + 1, 0), axis=1, keepdims=True)
    lane = lax.broadcasted_iota(jnp.int32, (slots, LANES), 1)
    extra = jnp.where(lane == 0, lax.shift_right_logical(tag, 6), jnp.where(lane == 1, tag & 63, 0))
    place = jnp.where(place, 1.0, 0.0).astype(jnp.bfloat16)
    for c in range(0, width, 512):
        part = jnp.dot(place, src[:, c:c + 512], preferred_element_type=jnp.float32).astype(jnp.bfloat16)
        sbuf[:, :, c:c + 512] = part.reshape(ndev, scap, 512)
    sbuf[:, :, width:] = extra.astype(jnp.float32).astype(jnp.bfloat16).reshape(ndev, scap, LANES)

    pl.semaphore_wait(barrier, ndev - 1)

    def block(a, b):
        return pltpu.make_async_remote_copy(
            src_ref=sbuf.at[a * rows + b], dst_ref=rbuf.at[me], send_sem=ssem, recv_sem=rsem,
            device_id=(a, b), device_id_type=MESH,
        )

    def post(t, _):
        a = lax.rem(t + i, cols)
        b = t // cols - a

        @pl.when((b >= 0) & (b < rows) & ((a != i) | (b != j)))
        def _():
            block(a, b).start()

        return 0

    lax.fori_loop(0, (cols + rows - 1) * cols, post, 0)
    own = pltpu.make_async_copy(sbuf.at[me], rbuf.at[me], lsem)
    own.start()

    slot = lax.broadcasted_iota(jnp.int32, (RCAP, ndev), 0)
    asked = jnp.where(slot < count[...], ret[...] + 1, 0)
    split = jnp.concatenate(
        [lax.shift_right_logical(asked, 6), asked & 63, jnp.zeros((ndev - 2 * RCAP, ndev), jnp.int32)], axis=0
    ).astype(jnp.float32)
    split = jnp.transpose(split).astype(jnp.bfloat16)
    asks = ndev * RCAP
    row = lax.broadcasted_iota(jnp.int32, (asks, ndev), 0)
    lane = lax.broadcasted_iota(jnp.int32, (asks, ndev), 1)
    place = row // RCAP
    owner = (place // BAND % cols) * rows + place // (BAND * cols) * BAND + place % BAND
    spread = jnp.where(lane == owner, 1.0, 0.0).astype(jnp.bfloat16)
    spread = jnp.dot(spread, split, preferred_element_type=jnp.float32)
    spread = jnp.where(lane == row % RCAP, spread * 64.0, jnp.where(lane == row % RCAP + RCAP, spread, 0.0))
    want[...] = jnp.sum(spread, axis=1, keepdims=True).astype(jnp.int32) - 1
    acc[...] = jnp.zeros_like(acc)

    @pl.when(i == 0)
    def _():
        xbuf[:, :face] = jnp.zeros((padded, face), jnp.bfloat16)

    @pl.when(j == 0)
    def _():
        xbuf[:, face:] = jnp.zeros((padded, face), jnp.bfloat16)

    own.wait()
    pltpu.make_async_copy(rbuf.at[pl.ds(0, ndev - 1)], rbuf.at[pl.ds(0, ndev - 1)], rsem).wait()
    for c in range(0, width, 512):
        w[width:, c:c + 512] = rbuf[:, :, c:c + 512].reshape(slots, 512)
    code = rbuf[:, :, width:].reshape(slots, LANES).astype(jnp.float32)
    code = jnp.transpose(code)
    shots[...] = (code[0:1, :] * 64.0 + code[1:2, :] - 1.0).astype(jnp.int32)
    load.wait()

    def right(k):
        at = pl.ds(pl.multiple_of(k * CHUNK, CHUNK), CHUNK)
        return pltpu.make_async_remote_copy(
            src_ref=traces.at[at, pl.ds(0, face)],
            dst_ref=xbuf.at[at, pl.ds(0, face)],
            send_sem=send_r.at[k],
            recv_sem=recv_r.at[k],
            device_id=(lax.rem(i + 1, cols), j),
            device_id_type=MESH,
        )

    def upper(k):
        at = pl.ds(pl.multiple_of(k * CHUNK, CHUNK), CHUNK)
        return pltpu.make_async_remote_copy(
            src_ref=traces.at[at, pl.ds(face, face)],
            dst_ref=xbuf.at[at, pl.ds(face, face)],
            send_sem=send_u.at[k],
            recv_sem=recv_u.at[k],
            device_id=(i, lax.rem(j + 1, rows)),
            device_id_type=MESH,
        )

    def step(k, _):
        at = pl.ds(pl.multiple_of(k * CHUNK, CHUNK), CHUNK)
        number = lax.broadcasted_iota(jnp.int32, (CHUNK, slots), 0) + k * CHUNK
        pick = jnp.where(number == shots[...], 1.0, 0.0).astype(jnp.bfloat16)

        extra = jnp.dot(pick, w[width:, :], preferred_element_type=jnp.float32)
        held[...] = extra

        @pl.when(i > 0)
        def _():
            right(k).wait_recv()

        @pl.when(j > 0)
        def _():
            upper(k).wait_recv()

        x = xbuf[at, :]
        term = jnp.dot(x, w[:width, face:], preferred_element_type=jnp.float32) + held[:, face:]
        traces[at, face:] = term.astype(jnp.bfloat16)

        @pl.when(j < rows - 1)
        def _():
            upper(k).start()

        term = jnp.dot(x, w[:width, :face], preferred_element_type=jnp.float32) + held[:, :face]
        traces[at, :face] = term.astype(jnp.bfloat16)

        @pl.when(i < cols - 1)
        def _():
            right(k).start()

        @pl.when(lax.rem(k, SPAN // CHUNK) == SPAN // CHUNK - 1)
        def _():
            first = pl.multiple_of((k // (SPAN // CHUNK)) * SPAN, SPAN)
            number = lax.broadcasted_iota(jnp.int32, (asks, SPAN), 1) + first
            pick = jnp.where(number == want[...], 1.0, 0.0).astype(jnp.bfloat16)
            for c in range(0, width, 256):
                got = jnp.dot(pick, traces[pl.ds(first, SPAN), c:c + 256], preferred_element_type=jnp.float32)
                acc[:, c:c + 256] += got.astype(jnp.bfloat16)

        return 0

    lax.fori_loop(0, chunks, step, 0)

    def answer(q, a, b):
        return pltpu.make_async_remote_copy(
            src_ref=gbuf.at[q], dst_ref=out.at[me], send_sem=gsem, recv_sem=osem,
            device_id=(a, b), device_id_type=MESH,
        )

    @pl.when((i == MARK) & (lax.rem(j, BAND) == BAND - 1))
    def _():
        def tell(p, _):
            @pl.when(p != me)
            def _():
                pl.semaphore_signal(
                    gate.at[j // BAND], inc=1, device_id=(p // rows, lax.rem(p, rows)), device_id_type=MESH
                )

            return 0

        lax.fori_loop(0, ndev, tell, 0)
        pl.semaphore_signal(gate.at[j // BAND], inc=1)

    last = total // SPAN * SPAN
    owners = BAND * cols
    number = lax.broadcasted_iota(jnp.int32, (owners * RCAP, total - last), 1) + last

    pl.semaphore_wait(gate.at[j // BAND], 1)

    def finish(g, _):
        rows_at = pl.ds(pl.multiple_of(g * owners * RCAP, owners * RCAP), owners * RCAP)
        pick = jnp.where(number == want[rows_at, :], 1.0, 0.0).astype(jnp.bfloat16)
        for c in range(0, width, 512):
            got = jnp.dot(pick, traces[last:total, c:c + 512], preferred_element_type=jnp.float32).astype(jnp.bfloat16)
            got = got + acc[rows_at, c:c + 512]
            gbuf[pl.ds(pl.multiple_of(g * owners, owners), owners), :, c:c + 512] = got.reshape(owners, RCAP, 512)
        @pl.when(g != j // BAND)
        def _():
            pl.semaphore_wait(gate.at[g], 1)


        def reply(q, _):
            t = lax.rem(q + me, owners)
            a = t // BAND
            b = g * BAND + lax.rem(t, BAND)

            @pl.when((a != i) | (b != j))
            def _():
                answer(g * owners + t, a, b).start()

            return 0

        lax.fori_loop(0, owners, reply, 0)
        return 0

    lax.fori_loop(0, rows // BAND, finish, 0)
    home = (j // BAND) * owners + i * BAND + lax.rem(j, BAND)
    mine = pltpu.make_async_copy(gbuf.at[home], out.at[me], psem)
    mine.start()

    def drain(k, _):
        @pl.when(j < rows - 1)
        def _():
            upper(k).wait_send()

        @pl.when(i < cols - 1)
        def _():
            right(k).wait_send()

        return 0

    lax.fori_loop(0, chunks, drain, 0)
    most = pl.ds(0, ndev - 1)
    pltpu.make_async_copy(sbuf.at[most], sbuf.at[most], ssem).wait()
    pltpu.make_async_copy(gbuf.at[most], gbuf.at[most], gsem).wait()
    mine.wait()
    pltpu.make_async_copy(out.at[most], out.at[most], osem).wait()


def body(trace_op, src_blocks, src_dest, src_shot, ret_shot, ret_count):
    cols = lax.axis_size("gx")
    rows = lax.axis_size("gy")
    ndev = cols * rows
    blk, width = src_blocks.shape
    total = 2048
    scap = 2
    vmem = pl.BlockSpec(memory_space=pltpu.VMEM)
    hbm = pl.BlockSpec(memory_space=pl.ANY)
    chunks = pl.cdiv(total, CHUNK)
    padded = chunks * CHUNK
    dma = pltpu.SemaphoreType.DMA
    arrived = pl.pallas_call(
        functools.partial(mega, cols, rows, total),
        out_shape=jax.ShapeDtypeStruct((ndev, RCAP, width), jnp.bfloat16),
        in_specs=[pl.BlockSpec(memory_space=pltpu.HBM), vmem, vmem, vmem, vmem, vmem],
        out_specs=hbm,
        scratch_shapes=[
            pltpu.VMEM((width + ndev * scap, width), jnp.bfloat16),
            pltpu.VMEM((padded, width), jnp.bfloat16),
            pltpu.VMEM((padded, width), jnp.bfloat16),
            pltpu.VMEM((ndev, scap, width + LANES), jnp.bfloat16),
            pltpu.VMEM((ndev, scap, width + LANES), jnp.bfloat16),
            pltpu.VMEM((ndev, RCAP, width), jnp.bfloat16),
            pltpu.VMEM((ndev * RCAP, width), jnp.bfloat16),
            pltpu.VMEM((ndev * RCAP, 1), jnp.int32),
            pltpu.VMEM((1, ndev * scap), jnp.int32),
            pltpu.VMEM((CHUNK, width), jnp.float32),
            pltpu.SemaphoreType.REGULAR((rows // BAND,)),
            dma, dma, dma, dma, dma, dma, dma,
            dma((chunks,)), dma((chunks,)), dma((chunks,)), dma((chunks,)),
        ],
        compiler_params=pltpu.CompilerParams(has_side_effects=True, collective_id=0, vmem_limit_bytes=50 * 1024 * 1024),
    )(
        trace_op.reshape(width, width),
        src_blocks,
        src_dest.reshape(1, blk),
        src_shot.reshape(1, blk),
        ret_shot.reshape(ndev, RCAP).T,
        ret_count.reshape(1, ndev),
    )
    return arrived.reshape(1, ndev, RCAP, width)


def solution(mesh):
    in_specs = (
        P("gx", "gy", None, None),
        P(("gx", "gy"), None),
        P(("gx", "gy"), None),
        P(("gx", "gy")),
        P(("gx", "gy"), None, None),
        P(("gx", "gy"), None),
    )
    out_specs = P(("gx", "gy"), None, None, None)
    return jax.shard_map(body, mesh=mesh, in_specs=in_specs, out_specs=out_specs, check_vma=False)
```
